32 devices in a mesh: mem: 2 (over x), col: 16 (over z, y, core).
Axes of the slice: x: 2, y: 2, z: 4, core: 2. Of those that a mesh axis runs over, the one named last changes fastest.
Arguments:
- perturbations: bfloat16 [2, 16, 384, 768], P('mem', None, 'col'), may hold values from -6 to 6
- gradient: float32 [16, 384, 768], P(None, 'col'), may hold values from -6 to 6
- member_weights: float32 [2], P('mem'), may hold values from 0.5 to 2
- scale_weights: float32 [3], replicated, may hold values from 0.2 to 2
- lon_filter: bfloat16 [3, 768, 768], P(None, 'mem'), may hold values from -1 to 1.5
- lat_filter: bfloat16 [3, 384, 384], P(None, 'col'), may hold values from -1 to 1.5
Outputs:
- increment: float32 [16, 384, 768], P('mem', 'col')
The draws below stay inside these ranges and needn't reach their ends.
All inputs are finite; a program needn't handle non-finite values.
Results may differ from the reference program's by a relative error of at most 0.01.
Values may be sent and summed in bfloat16 or wider, within the bound.
A program may use at most 64 MiB of HBM per device.

```python
import math
import jax
import jax.numpy as jnp
from jax import lax

NLON = 768
NLAT = 384
SCALES = 3
NLEV = 16
MEMBERS = 2


def banded(key, count, periodic):
    places = jnp.arange(count, dtype=jnp.float32)
    spacing = jnp.abs(places[:, None] - places[None, :])
    if periodic:
        spacing = jnp.minimum(spacing, count - spacing)
    lengths = [max(1.0, count / 96.0), count / 24.0, count / 6.0]
    filters = []
    for scale_index in range(3):
        key_shape, key_jitter = jax.random.split(jax.random.fold_in(key, 17 + scale_index))
        ratio = spacing / lengths[scale_index]
        kernel = jnp.exp(-0.5 * ratio * ratio)
        kernel = kernel * jax.random.uniform(key_shape, (count, count), jnp.float32, 0.5, 1.5)
        kernel = kernel / jnp.sum(kernel, axis=1, keepdims=True)
        spread = 0.5
        jitter = jnp.clip(jax.random.normal(key_jitter, (count, count), jnp.float32), -4.0, 4.0)
        filters.append(kernel + jitter * spread / jnp.sqrt(count * 1.0))
    return jnp.stack(filters).astype(jnp.bfloat16)


def draw_lon_filter(key, part):
    return banded(key, NLON, True)


def draw_lat_filter(key, part):
    return banded(key, NLAT, False)


def steps_of(rng, extent, cuts, smallest, high):
    factor_of, own = 1.0, jax.random.fold_in(rng, 6)
    for axis_at, parts in cuts:
        heights = jnp.exp(jax.random.uniform(jax.random.fold_in(own, axis_at), (parts,), jnp.float32, smallest / len(cuts), high / len(cuts)))
        factor_of = factor_of * jnp.repeat(heights, extent[axis_at] // parts).reshape([-1 if axis == axis_at else 1 for axis in range(len(extent))])
    return factor_of


def bell_draw(own_key, extent, deviation, most, shards=(), kind=jnp.bfloat16):
    loudness = steps_of(own_key, extent, shards, -0.22, 0.18) if shards else 1.0
    values = jax.random.normal(own_key, extent, jnp.float32) * deviation * loudness
    return jnp.minimum(jnp.maximum(values, -most), most).astype(kind)


def setup_inputs(seed: int = 0) -> dict:
    splits = jax.random.split(jax.random.key(seed), 7)
    return {
        "perturbations": bell_draw(splits[0], (MEMBERS, NLEV, NLAT, NLON), 1.0, 6.0, ((0, 2), (2, 16))),
        "gradient": bell_draw(splits[1], (NLEV, NLAT, NLON), 1.0, 6.0, ((1, 16),), jnp.float32),
        "member_weights": jnp.clip(jnp.exp(math.log(2.0) - 1.3862944 * jax.random.uniform(splits[2], (MEMBERS,), jnp.float32) ** steps_of(splits[2], (MEMBERS,), ((0, 2),), -0.2, 0.2)), 0.5, 2.0),
        "scale_weights": jnp.clip(jnp.exp(jax.random.uniform(splits[3], (SCALES,), jnp.float32, math.log(0.2), math.log(2.0))), 0.2, 2.0),
        "lon_filter": draw_lon_filter(jax.random.fold_in(splits[6], 71), 0),
        "lat_filter": draw_lat_filter(jax.random.fold_in(splits[6], 71), 0),
    }


def reference(perturbations, gradient, member_weights, scale_weights, lon_filter, lat_filter):
    lon_full = lon_filter.astype(jnp.float32)
    lat_full = lat_filter.astype(jnp.float32)

    def one_member(total, inputs):
        member, weight = inputs
        member_full = member.astype(jnp.float32)
        schur = (member_full * gradient).astype(jnp.bfloat16)
        along = jnp.einsum('laj,sij->lsai', schur.astype(jnp.float32), lon_full).astype(jnp.bfloat16)
        across = jnp.einsum('sab,lsbi->lsai', lat_full, along.astype(jnp.float32))
        filtered = jnp.einsum('s,lsai->lai', scale_weights, across).astype(jnp.bfloat16)
        return total + weight * member_full * filtered.astype(jnp.float32), None

    start = jnp.zeros(gradient.shape, jnp.float32)
    total, unused = lax.scan(one_member, start, (perturbations, member_weights))
    return total
```

```python
import functools

import jax
import jax.numpy as jnp
from jax import lax
from jax.experimental import pallas as pl
from jax.experimental.pallas import tpu as pltpu
from jax.sharding import PartitionSpec as P

MESH = pl.DeviceIdType.MESH
CORES = 2


def on_device(perturbations, gradient, member_weights, scale_weights, lon_filter, lat_filter):
    member = perturbations[0].astype(jnp.float32)
    schur = (member * gradient).astype(jnp.bfloat16)
    levels = lax.all_to_all(schur, "col", split_axis=0, concat_axis=1, tiled=True)
    along = jnp.einsum(
        "laj,sij->lsai",
        levels,
        lax.all_gather(lon_filter, "mem", axis=1, tiled=True),
        preferred_element_type=jnp.float32,
    ).astype(jnp.bfloat16)
    across = jnp.einsum(
        "sab,lsbi->lsai",
        lax.all_gather(lat_filter, "col", axis=1, tiled=True),
        along,
        preferred_element_type=jnp.float32,
    )
    filtered = jnp.einsum("s,lsai->lai", scale_weights, across).astype(jnp.bfloat16)
    back = lax.all_to_all(filtered, "col", split_axis=1, concat_axis=0, tiled=True)
    terms = member_weights[0] * member * back.astype(jnp.float32)
    return lax.psum_scatter(terms, "mem", scatter_dimension=0, tiled=True)


def fused(
    mems, cols, depth_z, pert_h, grad_h, mw, sw, lon_h, lat_h, out_h,
    pert, grad, lon, lonr, schur, xr, xs, latr, latf, latb, zs, ff, fb, back, acc, tsend, trecv,
    loads, lat_send, lat_recv, x_send, x_recv, lonx_send, lonx_recv, lons_send, lons_recv,
    b_send, b_recv, t_send, t_recv, stores,
):
    levels, rows, _ = grad.shape
    scales = lon.shape[0]
    half = pert.shape[3]
    group = levels // mems
    m, me = lax.axis_index("mem"), lax.axis_index("col")
    other = 1 - m
    depth_y = cols // CORES // depth_z
    q = lax.rem(me, CORES)
    yi = lax.rem(me // CORES, depth_y)
    zi = me // (CORES * depth_y)
    sibling = me + 1 - 2 * q

    def place(z, y, core):
        return (z * depth_y + y) * CORES + core

    def remote(src, dst, ssem, rsem, device):
        return pltpu.make_async_remote_copy(
            src_ref=src, dst_ref=dst, send_sem=ssem, recv_sem=rsem,
            device_id=device, device_id_type=MESH,
        )

    lat_load = pltpu.make_async_copy(lat_h, latr.at[me], loads.at[0])
    lat_load.start()
    pert_loads = [
        pltpu.make_async_copy(pert_h.at[0, :, :, pl.ds(h * half, half)], pert.at[h], loads.at[1 + h])
        for h in range(2)
    ]
    grad_load = pltpu.make_async_copy(grad_h, grad, loads.at[3])
    lon_load = pltpu.make_async_copy(lon_h, lon, loads.at[4])
    for load in pert_loads:
        load.start()
    grad_load.start()
    lon_load.start()

    barrier = pltpu.get_barrier_semaphore()

    def greet(d, carry):
        peer = lax.rem(me + d, cols)
        pl.semaphore_signal(barrier, inc=1, device_id=(m, peer), device_id_type=MESH)
        return carry

    lax.fori_loop(1, cols, greet, 0)
    pl.semaphore_signal(barrier, inc=1, device_id=(other, me), device_id_type=MESH)

    for load in pert_loads:
        load.wait()
    grad_load.wait()

    def product(c, carry):
        lev = lax.rem(c, mems) * group + c // mems
        for h in range(2):
            at = pl.ds(h * half, half)
            schur[c, :, at] = (
                pert[h, lev].astype(jnp.float32) * grad[lev, :, at]
            ).astype(jnp.bfloat16)
        return carry

    lax.fori_loop(0, cols, product, 0)
    lat_load.wait()
    pl.semaphore_wait(barrier, cols)

    lat_copies = []

    def lat_push(c, peer):
        copy = remote(
            latr.at[c], latr.at[c], lat_send.at[len(lat_copies)], lat_recv.at[c], (m, peer)
        )
        copy.start()
        lat_copies.append(copy)

    def lat_arrived(c):
        remote(latr.at[c], latr.at[c], lat_send.at[0], lat_recv.at[c], (m, sibling)).wait_recv()

    for dz in range(1, depth_z):
        lat_push(me, place(lax.rem(zi + dz, depth_z), yi, q))
    for dy in range(1, depth_y):
        lat_push(me, place(zi, lax.rem(yi + dy, depth_y), q))
    lat_push(me, sibling)

    def lon_push(s):
        return remote(
            lon_h.at[s, q], lonr.at[s, q], lonx_send.at[s], lonx_recv.at[s], (other, me)
        )

    for s in range(scales):
        lon_push(s).start()

    def x_push(k):
        peer = lax.rem(me + 1 + lax.rem(k + cols // 2 - 1, cols - 1), cols)
        return peer, remote(
            schur.at[peer], xr.at[me], x_send.at[peer], x_recv.at[me], (m, peer)
        )

    def x_start(k, carry):
        x_push(k)[1].start()
        return carry

    lax.fori_loop(0, cols - 1, x_start, 0)

    for dz in range(1, depth_z):
        c = place(lax.rem(zi + dz, depth_z), yi, q)
        lat_arrived(c)
        for dy in range(1, depth_y):
            lat_push(c, place(zi, lax.rem(yi + dy, depth_y), q))
        lat_push(c, sibling)
    for dz in range(depth_z):
        for dy in range(1, depth_y):
            c = place(lax.rem(zi + dz, depth_z), lax.rem(yi + dy, depth_y), q)
            lat_arrived(c)
            lat_push(c, sibling)
    for k in range(cols // CORES):
        lat_arrived(k * CORES + 1 - q)
    for c in range(cols):
        for s in range(scales):
            latf[s, c * rows:(c + 1) * rows, :] = latr[c, s].astype(jnp.float32)
    for s in range(scales):
        latb[s] = latf[s].astype(jnp.bfloat16)

    def lon_pass(s):
        return remote(
            lonr.at[s, q], lonr.at[s, q], lons_send.at[s], lons_recv.at[s], (m, sibling)
        )

    def lon_forward(s):
        lon_push(s).wait_recv()
        lon_pass(s).start()

    lon_forward(0)

    xr[me] = schur[me]

    def x_wait(k, carry):
        peer = lax.rem(me + 1 + k, cols)
        remote(schur.at[peer], xr.at[peer], x_send.at[peer], x_recv.at[peer], (m, peer)).wait_recv()
        return carry

    lax.fori_loop(0, cols - 1, x_wait, 0)
    for c in range(cols):
        ff[c * rows:(c + 1) * rows, :] = xr[c].astype(jnp.float32)
    xs[...] = ff[...].astype(jnp.bfloat16)
    for s in range(scales):
        zs[s] = (
            jnp.dot(latb[s], xs[...], preferred_element_type=jnp.float32) * sw[s]
        ).astype(jnp.bfloat16)

    def b_push(ih, k):
        peer = lax.rem(me + 1 + lax.rem(k + cols // 2 - 1, cols - 1), cols)
        return remote(
            fb.at[ih, peer], back.at[ih, me], b_send.at[ih, peer], b_recv.at[ih, me], (m, peer)
        )

    def filter_half(ih, source):
        total = None
        for s in range(scales):
            part = lax.dot_general(
                zs[s], source[s].reshape(half, 2 * half), (((1,), (1,)), ((), ())),
                preferred_element_type=jnp.float32,
            )
            total = part if total is None else total + part
        for c in range(cols):
            fb[ih, c] = total[c * rows:(c + 1) * rows, :].astype(jnp.bfloat16)
        back[ih, me] = fb[ih, me]

        def b_start(k, carry):
            b_push(ih, k).start()
            return carry

        lax.fori_loop(0, cols - 1, b_start, 0)

    lon_load.wait()
    filter_half(m, lon)
    for s in range(1, scales):
        lon_forward(s)
    for s in range(scales):
        remote(
            lonr.at[s, 1 - q], lonr.at[s, 1 - q], lons_send.at[s], lons_recv.at[s], (m, sibling)
        ).wait_recv()
    filter_half(other, lonr)

    weight = mw[0]

    def t_copy(ih, r):
        return remote(
            tsend.at[ih, r], trecv.at[ih, r], t_send.at[ih, r], t_recv.at[ih, r], (other, me)
        )

    for step in range(2):
        ih = m if step == 0 else other

        def term(c, lev, ih=ih):
            @pl.when(c != me)
            def _():
                remote(
                    fb.at[ih, c], back.at[ih, c], b_send.at[ih, c], b_recv.at[ih, c], (m, c)
                ).wait_recv()

            return weight * pert[ih, lev].astype(jnp.float32) * back[ih, c].astype(jnp.float32)

        def sent(r, carry, ih=ih, term=term):
            tsend[ih, r] = term(r * mems + other, other * group + r).astype(jnp.bfloat16)
            t_copy(ih, r).start()
            return carry

        def kept(r, carry, ih=ih, term=term):
            acc[r, :, pl.ds(pl.multiple_of(ih * half, 128), half)] = term(
                r * mems + m, m * group + r
            )
            return carry

        lax.fori_loop(0, group, sent, 0)
        lax.fori_loop(0, group, kept, 0)

    def finish(r, carry):
        for h in range(2):
            t_copy(h, r).wait_recv()
            at = pl.ds(h * half, half)
            acc[r, :, at] = acc[r, :, at] + trecv[h, r].astype(jnp.float32)
        pltpu.make_async_copy(acc.at[r], out_h.at[r], stores.at[r]).start()
        return carry

    lax.fori_loop(0, group, finish, 0)

    for copy in lat_copies:
        copy.wait_send()
    for s in range(scales):
        lon_push(s).wait_send()
        lon_pass(s).wait_send()

    def drain(k, carry):
        x_push(k)[1].wait_send()
        for ih in range(2):
            b_push(ih, k).wait_send()
        return carry

    lax.fori_loop(0, cols - 1, drain, 0)

    def drain_terms(r, carry):
        for h in range(2):
            t_copy(h, r).wait_send()
        pltpu.make_async_copy(acc.at[r], out_h.at[r], stores.at[r]).wait()
        return carry

    lax.fori_loop(0, group, drain_terms, 0)


def kernel_form(mems, cols, perturbations, gradient, member_weights, scale_weights, lon_filter, lat_filter):
    levels, rows, nlon = gradient.shape
    scales, lon_rows, _ = lon_filter.shape
    nlat = lat_filter.shape[2]
    half = nlon // 2
    group = levels // mems
    chips = cols // CORES
    depth_z = 4 if chips % 4 == 0 else 1
    depth_y = chips // depth_z
    lat_sends = (depth_z - 1) + (depth_y - 1) + 1 + (depth_z - 1) * depth_y + depth_z * (depth_y - 1)
    dma = pltpu.SemaphoreType.DMA
    bf, f32 = jnp.bfloat16, jnp.float32
    anywhere = pl.BlockSpec(memory_space=pl.ANY)
    scalars = pl.BlockSpec(memory_space=pltpu.SMEM)
    return pl.pallas_call(
        functools.partial(fused, mems, cols, depth_z),
        out_shape=jax.ShapeDtypeStruct((group, rows, nlon), f32),
        in_specs=[anywhere, anywhere, scalars, scalars, anywhere, anywhere],
        out_specs=anywhere,
        scratch_shapes=[
            pltpu.VMEM((2, levels, rows, half), bf),
            pltpu.VMEM((levels, rows, nlon), f32),
            pltpu.VMEM((scales, 2, lon_rows // 2, nlon), bf),
            pltpu.VMEM((scales, 2, lon_rows // 2, nlon), bf),
            pltpu.VMEM((cols, rows, nlon), bf),
            pltpu.VMEM((cols, rows, nlon), bf),
            pltpu.VMEM((nlat, nlon), bf),
            pltpu.VMEM((cols, scales, rows, nlat), bf),
            pltpu.VMEM((scales, nlat, nlat), f32),
            pltpu.VMEM((scales, nlat, nlat), bf),
            pltpu.VMEM((scales, nlat, nlon), bf),
            pltpu.VMEM((nlat, nlon), f32),
            pltpu.VMEM((2, cols, rows, half), bf),
            pltpu.VMEM((2, cols, rows, half), bf),
            pltpu.VMEM((group, rows, nlon), f32),
            pltpu.VMEM((2, group, rows, half), bf),
            pltpu.VMEM((2, group, rows, half), bf),
            dma((5,)), dma((lat_sends,)), dma((cols,)), dma((cols,)), dma((cols,)),
            dma((scales,)), dma((scales,)), dma((scales,)), dma((scales,)),
            dma((2, cols)), dma((2, cols)), dma((2, group)), dma((2, group)), dma((group,)),
        ],
        compiler_params=pltpu.CompilerParams(
            collective_id=0, has_side_effects=True, vmem_limit_bytes=48 * 1024 * 1024
        ),
    )(
        perturbations, gradient, member_weights, scale_weights,
        lon_filter.reshape(scales, 2, lon_rows // 2, nlon), lat_filter,
    )


def solution(mesh):
    mems, cols = mesh.shape["mem"], mesh.shape["col"]

    def step(perturbations, gradient, *rest):
        levels, rows, nlon = gradient.shape
        fits = mems == 2 and levels == cols and rows % 8 == 0 and nlon % 256 == 0
        if not fits:
            return on_device(perturbations, gradient, *rest)
        return kernel_form(mems, cols, perturbations, gradient, *rest)

    placed = (
        P("mem", None, "col", None),
        P(None, "col", None),
        P("mem"),
        P(),
        P(None, "mem", None),
        P(None, "col", None),
    )
    return jax.shard_map(
        step, mesh=mesh, in_specs=placed, out_specs=P("mem", "col", None), check_vma=False
    )
```

```python
import functools

import jax
import jax.numpy as jnp
from jax import lax
from jax.experimental import pallas as pl
from jax.experimental.pallas import tpu as pltpu
from jax.sharding import PartitionSpec as P

MESH = pl.DeviceIdType.MESH
CORES = 2


def on_device(perturbations, gradient, member_weights, scale_weights, lon_filter, lat_filter):
    member = perturbations[0].astype(jnp.float32)
    schur = (member * gradient).astype(jnp.bfloat16)
    levels = lax.all_to_all(schur, "col", split_axis=0, concat_axis=1, tiled=True)
    along = jnp.einsum(
        "laj,sij->lsai",
        levels,
        lax.all_gather(lon_filter, "mem", axis=1, tiled=True),
        preferred_element_type=jnp.float32,
    ).astype(jnp.bfloat16)
    across = jnp.einsum(
        "sab,lsbi->lsai",
        lax.all_gather(lat_filter, "col", axis=1, tiled=True),
        along,
        preferred_element_type=jnp.float32,
    )
    filtered = jnp.einsum("s,lsai->lai", scale_weights, across).astype(jnp.bfloat16)
    back = lax.all_to_all(filtered, "col", split_axis=1, concat_axis=0, tiled=True)
    terms = member_weights[0] * member * back.astype(jnp.float32)
    return lax.psum_scatter(terms, "mem", scatter_dimension=0, tiled=True)


def fused(
    mems, cols, depth_z, pert_h, grad_h, mw, sw, lon_h, lat_h, acc, trecv,
    pert, grad, lon, lonr, schur, xr, xs, latr, latf, latb, zs, ff, fb, back, tsend,
    loads, lat_send, lat_recv, x_send, x_recv, lonx_send, lonx_recv, lons_send, lons_recv,
    b_send, b_recv, t_send, t_recv,
):
    levels, rows, _ = grad.shape
    scales = lon.shape[0]
    half = pert.shape[3]
    group = levels // mems
    m, me = lax.axis_index("mem"), lax.axis_index("col")
    other = 1 - m
    depth_y = cols // CORES // depth_z
    q = lax.rem(me, CORES)
    yi = lax.rem(me // CORES, depth_y)
    zi = me // (CORES * depth_y)
    sibling = me + 1 - 2 * q

    def place(z, y, core):
        return (z * depth_y + y) * CORES + core

    def remote(src, dst, ssem, rsem, device):
        return pltpu.make_async_remote_copy(
            src_ref=src, dst_ref=dst, send_sem=ssem, recv_sem=rsem,
            device_id=device, device_id_type=MESH,
        )

    lat_load = pltpu.make_async_copy(lat_h, latr.at[me], loads.at[0])
    lat_load.start()
    pert_loads = [
        pltpu.make_async_copy(pert_h.at[0, :, :, pl.ds(h * half, half)], pert.at[h], loads.at[1 + h])
        for h in range(2)
    ]
    grad_load = pltpu.make_async_copy(grad_h, grad, loads.at[3])
    lon_load = pltpu.make_async_copy(lon_h, lon, loads.at[4])
    for load in pert_loads:
        load.start()
    grad_load.start()
    lon_load.start()

    barrier = pltpu.get_barrier_semaphore()

    def greet(d, carry):
        peer = lax.rem(me + d, cols)
        pl.semaphore_signal(barrier, inc=1, device_id=(m, peer), device_id_type=MESH)
        return carry

    lax.fori_loop(1, cols, greet, 0)
    pl.semaphore_signal(barrier, inc=1, device_id=(other, me), device_id_type=MESH)

    for load in pert_loads:
        load.wait()
    grad_load.wait()

    def product(c, carry):
        lev = lax.rem(c, mems) * group + c // mems
        for h in range(2):
            at = pl.ds(h * half, half)
            schur[h, c] = (
                pert[h, lev].astype(jnp.float32) * grad[lev, :, at]
            ).astype(jnp.bfloat16)
        return carry

    lax.fori_loop(0, cols, product, 0)
    lat_load.wait()
    pl.semaphore_wait(barrier, cols)

    lat_copies = []

    carrier = q == m

    def lat_push(c, device, when=None):
        copy = remote(
            latr.at[c], latr.at[c], lat_send.at[len(lat_copies)], lat_recv.at[c], device
        )
        lat_copies.append((copy, when))
        if when is None:
            copy.start()
        else:
            pl.when(when)(copy.start)

    def lat_arrived(c):
        remote(latr.at[c], latr.at[c], lat_send.at[0], lat_recv.at[c], (m, sibling)).wait_recv()

    for dz in range(1, depth_z):
        lat_push(me, (m, place(lax.rem(zi + dz, depth_z), yi, q)), carrier)
    for dy in range(1, depth_y):
        lat_push(me, (m, place(zi, lax.rem(yi + dy, depth_y), q)))
    lat_push(me, (m, sibling))

    def lon_push(s):
        return remote(
            lon_h.at[s, q], lonr.at[s, q], lonx_send.at[s], lonx_recv.at[s], (other, me)
        )

    lon_push(0).start()

    def x_push(h, k):
        peer = lax.rem(me + 1 + lax.rem(k + cols // 2 - 1, cols - 1), cols)
        return remote(
            schur.at[h, peer], xr.at[h, me], x_send.at[h, peer], x_recv.at[h, me], (m, peer)
        )

    for h in range(2):

        def x_start(k, carry, h=h):
            x_push(h, k).start()
            return carry

        lax.fori_loop(0, cols - 1, x_start, 0)

    for dz in range(1, depth_z):
        c = place(lax.rem(zi + dz, depth_z), yi, q)
        lat_arrived(c)
        lat_push(c, (other, me), carrier)
        for dy in range(1, depth_y):
            lat_push(c, (m, place(zi, lax.rem(yi + dy, depth_y), q)))
        lat_push(c, (m, sibling))
    for s in range(1, scales):
        lon_push(s).start()
    for dz in range(depth_z):
        for dy in range(1, depth_y):
            c = place(lax.rem(zi + dz, depth_z), lax.rem(yi + dy, depth_y), q)
            lat_arrived(c)
            lat_push(c, (m, sibling))
    for k in range(cols // CORES):
        lat_arrived(k * CORES + 1 - q)
    for c in range(cols):
        for s in range(scales):
            latf[s, c * rows:(c + 1) * rows, :] = latr[c, s].astype(jnp.float32)
    for s in range(scales):
        latb[s] = latf[s].astype(jnp.bfloat16)

    def lon_pass(s):
        return remote(
            lonr.at[s, q], lonr.at[s, q], lons_send.at[s], lons_recv.at[s], (m, sibling)
        )

    def lon_forward(s):
        lon_push(s).wait_recv()
        lon_pass(s).start()

    lon_forward(0)

    for h in range(2):
        xr[h, me] = schur[h, me]

        def x_wait(k, carry, h=h):
            peer = lax.rem(me + 1 + k, cols)
            remote(
                schur.at[h, peer], xr.at[h, peer], x_send.at[h, peer], x_recv.at[h, peer], (m, peer)
            ).wait_recv()
            return carry

        lax.fori_loop(0, cols - 1, x_wait, 0)
        at = pl.ds(h * half, half)
        for c in range(cols):
            ff[c * rows:(c + 1) * rows, at] = xr[h, c].astype(jnp.float32)
        xs[:, at] = ff[:, at].astype(jnp.bfloat16)
        for s in range(scales):
            zs[s, :, at] = (
                jnp.dot(latb[s], xs[:, at], preferred_element_type=jnp.float32) * sw[s]
            ).astype(jnp.bfloat16)

    def b_push(ih, k):
        peer = lax.rem(me + 1 + lax.rem(k + cols // 2 - 1, cols - 1), cols)
        return remote(
            fb.at[ih, peer], back.at[ih, me], b_send.at[ih, peer], b_recv.at[ih, me], (m, peer)
        )

    def filter_half(ih, source):
        total = None
        for s in range(scales):
            part = lax.dot_general(
                zs[s], source[s].reshape(half, 2 * half), (((1,), (1,)), ((), ())),
                preferred_element_type=jnp.float32,
            )
            total = part if total is None else total + part
        for c in range(cols):
            fb[ih, c] = total[c * rows:(c + 1) * rows, :].astype(jnp.bfloat16)
        back[ih, me] = fb[ih, me]

        def b_start(k, carry):
            b_push(ih, k).start()
            return carry

        lax.fori_loop(0, cols - 1, b_start, 0)

    lon_load.wait()
    filter_half(m, lon)
    for s in range(1, scales):
        lon_forward(s)
    for s in range(scales):
        remote(
            lonr.at[s, 1 - q], lonr.at[s, 1 - q], lons_send.at[s], lons_recv.at[s], (m, sibling)
        ).wait_recv()
    filter_half(other, lonr)

    weight = mw[0]

    def t_copy(ih, r):
        return remote(
            tsend.at[ih, r], trecv.at[r, :, pl.ds(pl.multiple_of(ih * half, 128), half)],
            t_send.at[ih, r], t_recv.at[ih, r], (other, me)
        )

    chips = cols // CORES

    def source_of(k, core):
        p, y = k // depth_y, lax.rem(yi + lax.rem(k, depth_y), depth_y)
        if depth_z == 4:
            low = lax.rem(p, 2)
            z = lax.rem(zi + low * (1 - 2 * lax.rem(zi, 2)) + 2 * (p // 2), depth_z)
        else:
            z = lax.rem(zi + p, depth_z)
        return place(z, y, core)

    def term(ih, c, lev):
        @pl.when(c != me)
        def _():
            remote(
                fb.at[ih, c], back.at[ih, c], b_send.at[ih, c], b_recv.at[ih, c], (m, c)
            ).wait_recv()

        return weight * pert[ih, lev].astype(jnp.float32) * back[ih, c].astype(jnp.float32)

    for ih in (m, other):

        def sent(k, carry, ih=ih):
            c = source_of(k, other)
            r = c // mems
            tsend[ih, r] = term(ih, c, other * group + r).astype(jnp.bfloat16)
            t_copy(ih, r).start()
            return carry

        lax.fori_loop(0, chips, sent, 0)

    for ih in (m, other):

        def kept(k, carry, ih=ih):
            c = source_of(k, m)
            r = c // mems
            acc[r, :, pl.ds(pl.multiple_of(ih * half, 128), half)] = term(ih, c, m * group + r)
            return carry

        lax.fori_loop(0, chips, kept, 0)

    def finish(r, carry):
        for h in range(2):
            t_copy(h, r).wait_recv()
        return carry

    lax.fori_loop(0, group, finish, 0)

    for copy, when in lat_copies:
        if when is None:
            copy.wait_send()
        else:
            pl.when(when)(copy.wait_send)
    for s in range(scales):
        lon_push(s).wait_send()
        lon_pass(s).wait_send()

    def drain(k, carry):
        for ih in range(2):
            x_push(ih, k).wait_send()
            b_push(ih, k).wait_send()
        return carry

    lax.fori_loop(0, cols - 1, drain, 0)

    def drain_terms(r, carry):
        for h in range(2):
            t_copy(h, r).wait_send()
        return carry

    lax.fori_loop(0, group, drain_terms, 0)


def kernel_form(mems, cols, perturbations, gradient, member_weights, scale_weights, lon_filter, lat_filter):
    levels, rows, nlon = gradient.shape
    scales, lon_rows, _ = lon_filter.shape
    nlat = lat_filter.shape[2]
    half = nlon // 2
    group = levels // mems
    chips = cols // CORES
    depth_z = 4 if chips % 4 == 0 else 1
    depth_y = chips // depth_z
    lat_sends = depth_z + depth_y - 1 + (depth_z - 1) * (depth_y + 1) + depth_z * (depth_y - 1)
    dma = pltpu.SemaphoreType.DMA
    bf, f32 = jnp.bfloat16, jnp.float32
    anywhere = pl.BlockSpec(memory_space=pltpu.MemorySpace.HBM)
    scalars = pl.BlockSpec(memory_space=pltpu.SMEM)
    own, received = pl.pallas_call(
        functools.partial(fused, mems, cols, depth_z),
        out_shape=[
            jax.ShapeDtypeStruct((group, rows, nlon), f32),
            jax.ShapeDtypeStruct((group, rows, nlon), bf),
        ],
        in_specs=[anywhere, anywhere, scalars, scalars, anywhere, anywhere],
        out_specs=[pl.BlockSpec(memory_space=pltpu.VMEM)] * 2,
        scratch_shapes=[
            pltpu.VMEM((2, levels, rows, half), bf),
            pltpu.VMEM((levels, rows, nlon), f32),
            pltpu.VMEM((scales, 2, lon_rows // 2, nlon), bf),
            pltpu.VMEM((scales, 2, lon_rows // 2, nlon), bf),
            pltpu.VMEM((2, cols, rows, half), bf),
            pltpu.VMEM((2, cols, rows, half), bf),
            pltpu.VMEM((nlat, nlon), bf),
            pltpu.VMEM((cols, scales, rows, nlat), bf),
            pltpu.VMEM((scales, nlat, nlat), f32),
            pltpu.VMEM((scales, nlat, nlat), bf),
            pltpu.VMEM((scales, nlat, nlon), bf),
            pltpu.VMEM((nlat, nlon), f32),
            pltpu.VMEM((2, cols, rows, half), bf),
            pltpu.VMEM((2, cols, rows, half), bf),
            pltpu.VMEM((2, group, rows, half), bf),
            dma((5,)), dma((lat_sends,)), dma((cols,)), dma((2, cols)), dma((2, cols)),
            dma((scales,)), dma((scales,)), dma((scales,)), dma((scales,)),
            dma((2, cols)), dma((2, cols)), dma((2, group)), dma((2, group)),
        ],
        compiler_params=pltpu.CompilerParams(
            collective_id=0, has_side_effects=True, vmem_limit_bytes=60 * 1024 * 1024
        ),
    )(
        perturbations, gradient, member_weights, scale_weights,
        lon_filter.reshape(scales, 2, lon_rows // 2, nlon), lat_filter,
    )
    return own + received.astype(f32)


def solution(mesh):
    mems, cols = mesh.shape["mem"], mesh.shape["col"]

    def step(perturbations, gradient, *rest):
        levels, rows, nlon = gradient.shape
        fits = mems == 2 and levels == cols and rows % 8 == 0 and nlon % 256 == 0
        if not fits:
            return on_device(perturbations, gradient, *rest)
        return kernel_form(mems, cols, perturbations, gradient, *rest)

    placed = (
        P("mem", None, "col", None),
        P(None, "col", None),
        P("mem"),
        P(),
        P(None, "mem", None),
        P(None, "col", None),
    )
    return jax.shard_map(
        step, mesh=mesh, in_specs=placed, out_specs=P("mem", "col", None), check_vma=False
    )
```

```python
import functools

import jax
import jax.numpy as jnp
from jax import lax
from jax.experimental import pallas as pl
from jax.experimental.pallas import tpu as pltpu
from jax.sharding import PartitionSpec as P

MESH = pl.DeviceIdType.MESH
CORES = 2


def on_device(perturbations, gradient, member_weights, scale_weights, lon_filter, lat_filter):
    member = perturbations[0].astype(jnp.float32)
    schur = (member * gradient).astype(jnp.bfloat16)
    levels = lax.all_to_all(schur, "col", split_axis=0, concat_axis=1, tiled=True)
    along = jnp.einsum(
        "laj,sij->lsai",
        levels,
        lax.all_gather(lon_filter, "mem", axis=1, tiled=True),
        preferred_element_type=jnp.float32,
    ).astype(jnp.bfloat16)
    across = jnp.einsum(
        "sab,lsbi->lsai",
        lax.all_gather(lat_filter, "col", axis=1, tiled=True),
        along,
        preferred_element_type=jnp.float32,
    )
    filtered = jnp.einsum("s,lsai->lai", scale_weights, across).astype(jnp.bfloat16)
    back = lax.all_to_all(filtered, "col", split_axis=1, concat_axis=0, tiled=True)
    terms = member_weights[0] * member * back.astype(jnp.float32)
    return lax.psum_scatter(terms, "mem", scatter_dimension=0, tiled=True)


def fused(
    mems, cols, depth_z, pert_h, grad_h, mw, sw, lon_h, lat_h, acc, trecv,
    pert, grad, lon, lonr, schur, xr, xs, latr, latf, latb, zs, ff, fb, back, tsend,
    loads, lat_send, lat_recv, x_send, x_recv, lonx_send, lonx_recv, lons_send, lons_recv,
    b_send, b_recv, t_send, t_recv,
):
    levels, rows, _ = grad.shape
    scales = lon.shape[0]
    half = pert.shape[3]
    group = levels // mems
    m, me = lax.axis_index("mem"), lax.axis_index("col")
    other = 1 - m
    depth_y = cols // CORES // depth_z
    q = lax.rem(me, CORES)
    yi = lax.rem(me // CORES, depth_y)
    zi = me // (CORES * depth_y)
    sibling = me + 1 - 2 * q

    def place(z, y, core):
        return (z * depth_y + y) * CORES + core

    def remote(src, dst, ssem, rsem, device):
        return pltpu.make_async_remote_copy(
            src_ref=src, dst_ref=dst, send_sem=ssem, recv_sem=rsem,
            device_id=device, device_id_type=MESH,
        )

    lat_load = pltpu.make_async_copy(lat_h, latr.at[me], loads.at[0])
    lat_load.start()
    pert_loads = [
        pltpu.make_async_copy(pert_h.at[0, :, :, pl.ds(h * half, half)], pert.at[h], loads.at[1 + h])
        for h in range(2)
    ]
    grad_load = pltpu.make_async_copy(grad_h, grad, loads.at[3])
    lon_load = pltpu.make_async_copy(lon_h, lon, loads.at[4])
    for load in pert_loads:
        load.start()
    grad_load.start()
    lon_load.start()

    barrier = pltpu.get_barrier_semaphore()

    def greet(d, carry):
        peer = lax.rem(me + 1 + lax.rem(d + cols // 2 - 2, cols - 1), cols)
        pl.semaphore_signal(barrier, inc=1, device_id=(m, peer), device_id_type=MESH)
        return carry

    lax.fori_loop(1, cols, greet, 0)
    pl.semaphore_signal(barrier, inc=1, device_id=(other, me), device_id_type=MESH)

    for load in pert_loads:
        load.wait()
    grad_load.wait()

    def product(c, carry):
        lev = lax.rem(c, mems) * group + c // mems
        for h in range(2):
            at = pl.ds(h * half, half)
            schur[h, c] = (
                pert[h, lev].astype(jnp.float32) * grad[lev, :, at]
            ).astype(jnp.bfloat16)
        return carry

    lax.fori_loop(0, cols, product, 0)
    lat_load.wait()
    pl.semaphore_wait(barrier, cols)

    lat_copies = []

    carrier = q == m

    def lat_push(c, device, when=None):
        copy = remote(
            latr.at[c], latr.at[c], lat_send.at[len(lat_copies)], lat_recv.at[c], device
        )
        lat_copies.append((copy, when))
        if when is None:
            copy.start()
        else:
            pl.when(when)(copy.start)

    def lat_arrived(c):
        remote(latr.at[c], latr.at[c], lat_send.at[0], lat_recv.at[c], (m, sibling)).wait_recv()

    for dz in range(1, depth_z):
        lat_push(me, (m, place(lax.rem(zi + dz, depth_z), yi, q)), carrier)
    for dy in range(1, depth_y):
        lat_push(me, (m, place(zi, lax.rem(yi + dy, depth_y), q)))
    lat_push(me, (m, sibling))

    def lon_push(s):
        return remote(
            lon_h.at[s, q], lonr.at[s, q], lonx_send.at[s], lonx_recv.at[s], (other, me)
        )

    lon_push(0).start()

    def x_push(h, k):
        peer = lax.rem(me + 1 + lax.rem(k + cols // 2 - 1, cols - 1), cols)
        return remote(
            schur.at[h, peer], xr.at[h, me], x_send.at[h, peer], x_recv.at[h, me], (m, peer)
        )

    for h in range(2):

        def x_start(k, carry, h=h):
            x_push(h, k).start()
            return carry

        lax.fori_loop(0, cols - 1, x_start, 0)

    for dz in range(1, depth_z):
        c = place(lax.rem(zi + dz, depth_z), yi, q)
        lat_arrived(c)
        lat_push(c, (other, me), carrier)
        for dy in range(1, depth_y):
            lat_push(c, (m, place(zi, lax.rem(yi + dy, depth_y), q)))
        lat_push(c, (m, sibling))
    for s in range(1, scales):
        lon_push(s).start()
    for dz in range(depth_z):
        for dy in range(1, depth_y):
            c = place(lax.rem(zi + dz, depth_z), lax.rem(yi + dy, depth_y), q)
            lat_arrived(c)
            lat_push(c, (m, sibling))
    for k in range(cols // CORES):
        lat_arrived(k * CORES + 1 - q)
    for c in range(cols):
        for s in range(scales):
            latf[s, c * rows:(c + 1) * rows, :] = latr[c, s].astype(jnp.float32)
    for s in range(scales):
        latb[s] = latf[s].astype(jnp.bfloat16)

    def lon_pass(s):
        return remote(
            lonr.at[s, q], lonr.at[s, q], lons_send.at[s], lons_recv.at[s], (m, sibling)
        )

    def lon_forward(s):
        lon_push(s).wait_recv()
        lon_pass(s).start()

    lon_forward(0)

    for h in range(2):
        xr[h, me] = schur[h, me]

        def x_wait(k, carry, h=h):
            peer = lax.rem(me + 1 + k, cols)
            remote(
                schur.at[h, peer], xr.at[h, peer], x_send.at[h, peer], x_recv.at[h, peer], (m, peer)
            ).wait_recv()
            return carry

        lax.fori_loop(0, cols - 1, x_wait, 0)
        at = pl.ds(h * half, half)
        for c in range(cols):
            ff[c * rows:(c + 1) * rows, at] = xr[h, c].astype(jnp.float32)
        xs[:, at] = ff[:, at].astype(jnp.bfloat16)
        for s in range(scales):
            zs[s, :, at] = (
                jnp.dot(latb[s], xs[:, at], preferred_element_type=jnp.float32) * sw[s]
            ).astype(jnp.bfloat16)

    def b_push(ih, k):
        peer = lax.rem(me + 1 + lax.rem(cols + cols // 2 - 2 - k, cols - 1), cols)
        return remote(
            fb.at[ih, peer], back.at[ih, me], b_send.at[ih, peer], b_recv.at[ih, me], (m, peer)
        )

    def filter_half(ih, source):
        total = None
        for s in range(scales):
            part = lax.dot_general(
                zs[s], source[s].reshape(half, 2 * half), (((1,), (1,)), ((), ())),
                preferred_element_type=jnp.float32,
            )
            total = part if total is None else total + part
        for c in range(cols):
            fb[ih, c] = total[c * rows:(c + 1) * rows, :].astype(jnp.bfloat16)
        back[ih, me] = fb[ih, me]

        def b_start(k, carry):
            b_push(ih, k).start()
            return carry

        lax.fori_loop(0, cols - 1, b_start, 0)

    lon_load.wait()
    filter_half(m, lon)
    for s in range(1, scales):
        lon_forward(s)
    for s in range(scales):
        remote(
            lonr.at[s, 1 - q], lonr.at[s, 1 - q], lons_send.at[s], lons_recv.at[s], (m, sibling)
        ).wait_recv()
    filter_half(other, lonr)

    weight = mw[0]

    def t_copy(ih, r):
        return remote(
            tsend.at[ih, r], trecv.at[r, :, pl.ds(pl.multiple_of(ih * half, 128), half)],
            t_send.at[ih, r], t_recv.at[ih, r], (other, me)
        )

    chips = cols // CORES

    def source_of(k, core):
        p, y = k // depth_y, lax.rem(yi + lax.rem(k, depth_y), depth_y)
        if depth_z == 4:
            low = lax.rem(p, 2)
            z = lax.rem(zi + low * (1 - 2 * lax.rem(zi, 2)) + 2 * (p // 2), depth_z)
        else:
            z = lax.rem(zi + p, depth_z)
        return place(z, y, core)

    def term(ih, c, lev):
        @pl.when(c != me)
        def _():
            remote(
                fb.at[ih, c], back.at[ih, c], b_send.at[ih, c], b_recv.at[ih, c], (m, c)
            ).wait_recv()

        return weight * pert[ih, lev].astype(jnp.float32) * back[ih, c].astype(jnp.float32)

    for ih in (m, other):

        def sent(k, carry, ih=ih):
            c = source_of(k, other)
            r = c // mems
            tsend[ih, r] = term(ih, c, other * group + r).astype(jnp.bfloat16)
            t_copy(ih, r).start()
            return carry

        lax.fori_loop(0, chips, sent, 0)

    for ih in (m, other):

        def kept(k, carry, ih=ih):
            c = source_of(k, m)
            r = c // mems
            acc[r, :, pl.ds(pl.multiple_of(ih * half, 128), half)] = term(ih, c, m * group + r)
            return carry

        lax.fori_loop(0, chips, kept, 0)

    def finish(r, carry):
        for h in range(2):
            t_copy(h, r).wait_recv()
        return carry

    lax.fori_loop(0, group, finish, 0)

    for copy, when in lat_copies:
        if when is None:
            copy.wait_send()
        else:
            pl.when(when)(copy.wait_send)
    for s in range(scales):
        lon_push(s).wait_send()
        lon_pass(s).wait_send()

    def drain(k, carry):
        for ih in range(2):
            x_push(ih, k).wait_send()
            b_push(ih, k).wait_send()
        return carry

    lax.fori_loop(0, cols - 1, drain, 0)

    def drain_terms(r, carry):
        for h in range(2):
            t_copy(h, r).wait_send()
        return carry

    lax.fori_loop(0, group, drain_terms, 0)


def kernel_form(mems, cols, perturbations, gradient, member_weights, scale_weights, lon_filter, lat_filter):
    levels, rows, nlon = gradient.shape
    scales, lon_rows, _ = lon_filter.shape
    nlat = lat_filter.shape[2]
    half = nlon // 2
    group = levels // mems
    chips = cols // CORES
    depth_z = 4 if chips % 4 == 0 else 1
    depth_y = chips // depth_z
    lat_sends = depth_z + depth_y - 1 + (depth_z - 1) * (depth_y + 1) + depth_z * (depth_y - 1)
    dma = pltpu.SemaphoreType.DMA
    bf, f32 = jnp.bfloat16, jnp.float32
    anywhere = pl.BlockSpec(memory_space=pltpu.MemorySpace.HBM)
    scalars = pl.BlockSpec(memory_space=pltpu.SMEM)
    own, received = pl.pallas_call(
        functools.partial(fused, mems, cols, depth_z),
        out_shape=[
            jax.ShapeDtypeStruct((group, rows, nlon), f32),
            jax.ShapeDtypeStruct((group, rows, nlon), bf),
        ],
        in_specs=[anywhere, anywhere, scalars, scalars, anywhere, anywhere],
        out_specs=[pl.BlockSpec(memory_space=pltpu.VMEM)] * 2,
        scratch_shapes=[
            pltpu.VMEM((2, levels, rows, half), bf),
            pltpu.VMEM((levels, rows, nlon), f32),
            pltpu.VMEM((scales, 2, lon_rows // 2, nlon), bf),
            pltpu.VMEM((scales, 2, lon_rows // 2, nlon), bf),
            pltpu.VMEM((2, cols, rows, half), bf),
            pltpu.VMEM((2, cols, rows, half), bf),
            pltpu.VMEM((nlat, nlon), bf),
            pltpu.VMEM((cols, scales, rows, nlat), bf),
            pltpu.VMEM((scales, nlat, nlat), f32),
            pltpu.VMEM((scales, nlat, nlat), bf),
            pltpu.VMEM((scales, nlat, nlon), bf),
            pltpu.VMEM((nlat, nlon), f32),
            pltpu.VMEM((2, cols, rows, half), bf),
            pltpu.VMEM((2, cols, rows, half), bf),
            pltpu.VMEM((2, group, rows, half), bf),
            dma((5,)), dma((lat_sends,)), dma((cols,)), dma((2, cols)), dma((2, cols)),
            dma((scales,)), dma((scales,)), dma((scales,)), dma((scales,)),
            dma((2, cols)), dma((2, cols)), dma((2, group)), dma((2, group)),
        ],
        compiler_params=pltpu.CompilerParams(
            collective_id=0, has_side_effects=True, vmem_limit_bytes=60 * 1024 * 1024
        ),
    )(
        perturbations, gradient, member_weights, scale_weights,
        lon_filter.reshape(scales, 2, lon_rows // 2, nlon), lat_filter,
    )
    return own + received.astype(f32)


def solution(mesh):
    mems, cols = mesh.shape["mem"], mesh.shape["col"]

    def step(perturbations, gradient, *rest):
        levels, rows, nlon = gradient.shape
        fits = mems == 2 and levels == cols and rows % 8 == 0 and nlon % 256 == 0
        if not fits:
            return on_device(perturbations, gradient, *rest)
        return kernel_form(mems, cols, perturbations, gradient, *rest)

    placed = (
        P("mem", None, "col", None),
        P(None, "col", None),
        P("mem"),
        P(),
        P(None, "mem", None),
        P(None, "col", None),
    )
    return jax.shard_map(
        step, mesh=mesh, in_specs=placed, out_specs=P("mem", "col", None), check_vma=False
    )
```
